32 devices in a mesh: tensor: 2 (over y), context: 16 (over z, x, core).
Axes of the slice: x: 2, y: 2, z: 4, core: 2. Of those that a mesh axis runs over, the one named last changes fastest.
Arguments:
- query_stream: bfloat16 [8192, 2048], P('tensor', 'context'), may hold values from -6 to 6
- key_stream: bfloat16 [8192, 2048], P('tensor', 'context'), may hold values from -6 to 6
- value_stream: bfloat16 [8192, 2048], P('tensor', 'context'), may hold values from -6 to 6
- filter_taps: bfloat16 [2048, 8192], P(('tensor', 'context')), may hold values from -0.125 to 0.125
- short_filters: float32 [3, 3, 8192], P(None, None, ('tensor', 'context')), may hold values from -3 to 3
- skip_gain: float32 [8192], P(('tensor', 'context')), may hold values from 0.5 to 1.5
Outputs:
- gated_out: bfloat16 [8192, 2048], P('tensor', 'context')
The draws below stay inside these ranges and needn't reach their ends.
All inputs are finite; a program needn't handle non-finite values.
Results may differ from the reference program's by a relative error of at most 0.0057.
Values may be sent and summed in bfloat16 or wider, within the bound.
A program may use at most 128 MiB of HBM per device.

```python
import jax
import jax.numpy as jnp
from jax import lax

D = 8192
SEQ = 2048


def levels(stream_key, dims, pieces, least, high):
    def one(position, shards_of):
        draws = jax.random.uniform(jax.random.fold_in(jax.random.fold_in(stream_key, 6), position), (shards_of,), jnp.float32, least / len(pieces), high / len(pieces))
        return jnp.repeat(jnp.exp(draws), dims[position] // shards_of).reshape((-1,) + (1,) * (len(dims) - position - 1))

    gain = one(*pieces[0])
    for cut in pieces[1:]:
        gain = gain * one(*cut)
    return gain


def gaussian(rng, extent, spread, reach, cuts=(), held_as=jnp.bfloat16):
    gain = levels(rng, extent, cuts, -0.22, 0.18) if cuts else 1.0
    array = jax.random.normal(rng, extent, jnp.float32) * spread * gain
    return jnp.minimum(jnp.maximum(array, -reach), reach).astype(held_as)


def setup_inputs(seed: int = 0) -> dict:
    key_of = jax.random.split(jax.random.key(seed), 7)
    return {
        "query_stream": gaussian(key_of[0], (D, SEQ), 1.0, 6.0, ((0, 2), (1, 16))),
        "key_stream": gaussian(key_of[1], (D, SEQ), 1.0, 6.0, ((0, 2), (1, 16))),
        "value_stream": gaussian(key_of[2], (D, SEQ), 1.0, 6.0, ((0, 2), (1, 16))),
        "filter_taps": gaussian(key_of[3], (SEQ, D), SEQ ** -0.5, 0.125, ((0, 32),)),
        "short_filters": gaussian(key_of[4], (3, 3, D), 0.6, 3.0, ((2, 32),), jnp.float32),
        "skip_gain": jnp.clip(0.5 + 1.0 * jax.random.uniform(key_of[5], (D,), jnp.float32) ** levels(key_of[5], (D,), ((0, 32),), -0.2, 0.2), 0.5, 1.5),
    }


def short_filter(signal, weights):
    padded = jnp.pad(signal, ((0, 0), (2, 0)))
    length = signal.shape[1]
    return (weights[0][:, None] * padded[:, 2:] + weights[1][:, None] * padded[:, 1:length + 1]
            + weights[2][:, None] * padded[:, :length])


def causal_block(paired):
    inputs, filters = paired
    length = inputs.shape[1]
    spectrum = jnp.fft.rfft(inputs, 2 * length, axis=1) * jnp.fft.rfft(filters, 2 * length, axis=1)
    return jnp.fft.irfft(spectrum, 2 * length, axis=1)[:, :length]


def reference(query_stream, key_stream, value_stream, filter_taps, short_filters, skip_gain):
    query_short = short_filter(query_stream.astype(jnp.float32), short_filters[0])
    key_short = short_filter(key_stream.astype(jnp.float32), short_filters[1])
    value_short = short_filter(value_stream.astype(jnp.float32), short_filters[2])
    products = lax.optimization_barrier((key_short * value_short).astype(jnp.bfloat16)).astype(jnp.float32)
    block_count = D // 256
    filters = filter_taps.astype(jnp.float32).T
    convolved = lax.map(causal_block, (products.reshape(block_count, 256, SEQ), filters.reshape(block_count, 256, SEQ)))
    convolved = convolved.reshape(D, SEQ)
    mixed_out = lax.optimization_barrier((convolved + skip_gain[:, None] * products).astype(jnp.bfloat16)).astype(jnp.float32)
    return (query_short * mixed_out).astype(jnp.bfloat16)
```

```python
import functools

import jax
import jax.numpy as jnp
import ml_dtypes
import numpy as np
from jax import lax
from jax.experimental import pallas as pl
from jax.experimental.pallas import tpu as pltpu
from jax.sharding import PartitionSpec as P

F32, BF16 = jnp.float32, jnp.bfloat16


def split(table):
    high = table.astype(ml_dtypes.bfloat16)
    low = (table - high.astype(np.float64)).astype(ml_dtypes.bfloat16)
    return jnp.asarray(high), jnp.asarray(low)


def tables(block):
    n = np.arange(2 * block)
    f = np.arange(block)
    phase = (n[:, None] * (2 * f[None, :] + 1)) % (4 * block)
    angle = phase * (2.0 * np.pi / (4 * block))
    forward = np.concatenate([np.cos(angle), -np.sin(angle)], axis=1)
    inverse = forward[block:].T / block
    return split(forward), split(inverse)


def params(**kw):
    return pltpu.CompilerParams(vmem_limit_bytes=60 * 1024 * 1024, **kw)


def rim_kernel(q_ref, k_ref, v_ref, out_ref):
    width = q_ref.shape[1]
    row = lax.broadcasted_iota(jnp.int32, (8, width), 0)
    col = lax.broadcasted_iota(jnp.int32, (8, width), 1)
    total = None
    for stream, ref in enumerate((q_ref, k_ref, v_ref)):
        pick = jnp.where(
            (row >= 2 * stream) & (row < 2 * stream + 2) & (col == width - 2 + row - 2 * stream), 1.0, 0.0
        ).astype(BF16)
        part = lax.dot_general(pick, ref[...], (((1,), (1,)), ((), ())), preferred_element_type=F32)
        total = part if total is None else total + part
    out_ref[0] = total.astype(BF16)


def columns(weights_ref, rim_ref):
    weights = weights_ref[0]
    rim = rim_ref[0].astype(F32)
    rest = jnp.zeros((128 - weights.shape[0] - rim.shape[0], weights.shape[1]), F32)
    return jnp.concatenate([weights, rim, rest], axis=0).T


def short_filter(signal, table, stream):
    signal = signal.astype(F32)
    at = lambda k: table[:, k : k + 1]
    lane = lax.broadcasted_iota(jnp.int32, signal.shape, 1)
    before2, before1 = at(16 + 2 * stream), at(17 + 2 * stream)
    lag1 = jnp.where(lane == 0, before1, pltpu.roll(signal, 1, 1))
    lag2 = jnp.where(lane == 0, before2, jnp.where(lane == 1, before1, pltpu.roll(signal, 2, 1)))
    return at(3 * stream) * signal + at(3 * stream + 1) * lag1 + at(3 * stream + 2) * lag2


def products_kernel(k_ref, v_ref, weights_ref, rim_ref, out_ref):
    table = columns(weights_ref, rim_ref)
    out_ref[...] = (short_filter(k_ref[...], table, 1) * short_filter(v_ref[...], table, 2)).astype(BF16)


def query_kernel(q_ref, weights_ref, rim_ref, out_ref):
    out_ref[...] = short_filter(q_ref[...], columns(weights_ref, rim_ref), 0)


def taps_kernel(h_ref, high_ref, low_ref, out_ref):
    block = h_ref.shape[0]
    dims = (((0,), (0,)), ((), ()))
    h = h_ref[...]
    out_ref[0] = lax.dot_general(h, high_ref[:block], dims, preferred_element_type=F32) + lax.dot_general(
        h, low_ref[:block], dims, preferred_element_type=F32
    )


def conv_kernel(x_ref, h_ref, skip_ref, high_ref, low_ref, back_high_ref, back_low_ref, out_ref, spec_ref, mixed_ref):
    pieces, chans, width = x_ref.shape
    blocks = pieces // 2
    half = 2 * width
    zero = jnp.zeros((chans, width), BF16)
    piece = lambda p: zero if p < 0 else x_ref[p]
    parts = [jnp.concatenate([piece(2 * j - 2 + lag) for j in range(blocks)], axis=0) for lag in range(4)]
    stacked = jnp.concatenate(parts, axis=1)
    spec_ref[...] = jnp.dot(stacked, high_ref[...], preferred_element_type=F32) + jnp.dot(
        stacked, low_ref[...], preferred_element_type=F32
    )

    @pl.loop(0, chans // 8)
    def _(group):
        base = pl.multiple_of(group * 8, 8)
        for lanes in range(half // 128):
            real, imag = pl.ds(lanes * 128, 128), pl.ds(half + lanes * 128, 128)
            rows = [pl.ds(pl.multiple_of(j * chans + base, 8), 8) for j in range(blocks)]
            xr = [spec_ref[r, real] for r in rows]
            xi = [spec_ref[r, imag] for r in rows]
            hr = [h_ref[j, pl.ds(base, 8), real] for j in range(blocks)]
            hi = [h_ref[j, pl.ds(base, 8), imag] for j in range(blocks)]
            for i in range(blocks):
                yr = xr[i] * hr[0] - xi[i] * hi[0]
                yi = xr[i] * hi[0] + xi[i] * hr[0]
                for j in range(i):
                    d = i - j
                    yr = yr + xr[j] * hr[d] - xi[j] * hi[d]
                    yi = yi + xr[j] * hi[d] + xi[j] * hr[d]
                mixed_ref[rows[i], real] = yr
                mixed_ref[rows[i], imag] = yi

    spectrum = mixed_ref[...]
    top = spectrum.astype(BF16)
    rest = (spectrum - top.astype(F32)).astype(BF16)
    conv = (
        jnp.dot(top, back_high_ref[...], preferred_element_type=F32)
        + jnp.dot(rest, back_high_ref[...], preferred_element_type=F32)
        + jnp.dot(top, back_low_ref[...], preferred_element_type=F32)
    )
    skip = skip_ref[...]
    for j in range(blocks):
        for side in range(2):
            part = conv[j * chans : (j + 1) * chans, side * width : (side + 1) * width]
            out_ref[2 * j + side] = (part + skip * x_ref[2 * j + side].astype(F32)).astype(BF16)


def local(query_stream, key_stream, value_stream, filter_taps, short_filters, skip_gain):
    group_width, block_rows = query_stream.shape
    context_size = lax.axis_size("context")
    tensor_size = lax.axis_size("tensor")
    everyone = tensor_size * context_size
    chans = group_width // context_size
    offset_rows = filter_taps.shape[0]
    block = 2 * block_rows
    blocks = context_size // 2
    (high, low), (back_high, back_low) = tables(block)

    grid = (context_size,)
    stream_spec = pl.BlockSpec((chans, block_rows), lambda i: (i, 0))
    weights_spec = pl.BlockSpec((1, 16, chans), lambda i: (i, 0, 0))
    rim_spec = pl.BlockSpec((1, 8, chans), lambda i: (i, 0, 0))

    weights = jnp.pad(short_filters.reshape(9, chans), ((0, 7), (0, 0)))
    weights = jnp.broadcast_to(weights[None], (context_size, 16, chans))
    weights = lax.all_to_all(weights, "context", split_axis=0, concat_axis=0, tiled=True)

    rim = pl.pallas_call(
        rim_kernel,
        grid=grid,
        in_specs=[stream_spec] * 3,
        out_specs=rim_spec,
        out_shape=jax.ShapeDtypeStruct((context_size, 8, chans), BF16),
        compiler_params=params(),
        cost_estimate=pl.CostEstimate(flops=0, bytes_accessed=6 * group_width * block_rows, transcendentals=0),
    )(query_stream, key_stream, value_stream)
    rim = lax.ppermute(rim, "context", [(s, s + 1) for s in range(context_size - 1)])

    sent = filter_taps.reshape(offset_rows, everyone, chans).transpose(1, 0, 2)
    taps = lax.all_to_all(sent, ("tensor", "context"), split_axis=0, concat_axis=0, tiled=True)
    taps = taps.reshape(everyone * offset_rows, chans)

    products = pl.pallas_call(
        products_kernel,
        grid=grid,
        in_specs=[stream_spec, stream_spec, weights_spec, rim_spec],
        out_specs=stream_spec,
        out_shape=jax.ShapeDtypeStruct((group_width, block_rows), BF16),
        compiler_params=params(),
        cost_estimate=pl.CostEstimate(flops=0, bytes_accessed=6 * group_width * block_rows, transcendentals=0),
    )(key_stream, value_stream, weights, rim)
    arrived = lax.all_to_all(
        products.reshape(context_size, chans, block_rows), "context", split_axis=0, concat_axis=0, tiled=True
    )

    whole2 = lambda rows, cols: pl.BlockSpec((rows, cols), lambda i: (0, 0))
    taps_spec = pl.pallas_call(
        taps_kernel,
        grid=(blocks,),
        in_specs=[pl.BlockSpec((block, chans), lambda i: (i, 0)), whole2(block, 2 * block), whole2(block, 2 * block)],
        out_specs=pl.BlockSpec((1, chans, 2 * block), lambda i: (i, 0, 0)),
        out_shape=jax.ShapeDtypeStruct((blocks, chans, 2 * block), F32),
        compiler_params=params(),
        cost_estimate=pl.CostEstimate(
            flops=8 * blocks * block * block * chans, bytes_accessed=10 * blocks * block * chans, transcendentals=0
        ),
    )(taps, high, low)

    step = min(chans, 64)
    mixed = pl.pallas_call(
        conv_kernel,
        grid=(chans // step,),
        in_specs=[
            pl.BlockSpec((context_size, step, block_rows), lambda i: (0, i, 0)),
            pl.BlockSpec((blocks, step, 2 * block), lambda i: (0, i, 0)),
            pl.BlockSpec((step, 1), lambda i: (i, 0)),
            whole2(2 * block, 2 * block),
            whole2(2 * block, 2 * block),
            whole2(2 * block, block),
            whole2(2 * block, block),
        ],
        out_specs=pl.BlockSpec((context_size, step, block_rows), lambda i: (0, i, 0)),
        out_shape=jax.ShapeDtypeStruct((context_size, chans, block_rows), BF16),
        scratch_shapes=[pltpu.VMEM((blocks * step, 2 * block), F32)] * 2,
        compiler_params=params(),
    )(arrived, taps_spec, skip_gain[:, None], high, low, back_high, back_low)
    returned = lax.all_to_all(mixed, "context", split_axis=0, concat_axis=0, tiled=True)

    query_short = pl.pallas_call(
        query_kernel,
        grid=grid,
        in_specs=[stream_spec, weights_spec, rim_spec],
        out_specs=stream_spec,
        out_shape=jax.ShapeDtypeStruct((group_width, block_rows), F32),
        compiler_params=params(),
        cost_estimate=pl.CostEstimate(flops=0, bytes_accessed=6 * group_width * block_rows, transcendentals=0),
    )(query_stream, weights, rim)
    return (query_short * returned.reshape(group_width, block_rows).astype(F32)).astype(BF16)


def solution(mesh):
    placed = (
        P("tensor", "context"),
        P("tensor", "context"),
        P("tensor", "context"),
        P(("tensor", "context"), None),
        P(None, None, ("tensor", "context")),
        P(("tensor", "context")),
    )
    return jax.shard_map(
        local, mesh=mesh, in_specs=placed, out_specs=P("tensor", "context"), check_vma=False
    )
```

```python
import functools

import jax
import jax.numpy as jnp
import ml_dtypes
import numpy as np
from jax import lax
from jax.experimental import pallas as pl
from jax.experimental.pallas import tpu as pltpu
from jax.sharding import PartitionSpec as P

F32, BF16 = jnp.float32, jnp.bfloat16
MESH = pl.DeviceIdType.MESH


def split(table):
    high = table.astype(ml_dtypes.bfloat16)
    low = (table - high.astype(np.float64)).astype(ml_dtypes.bfloat16)
    return jnp.asarray(high), jnp.asarray(low)


def tables(block):
    n = np.arange(2 * block)
    f = np.arange(block)
    phase = (n[:, None] * (2 * f[None, :] + 1)) % (4 * block)
    angle = phase * (2.0 * np.pi / (4 * block))
    forward = np.concatenate([np.cos(angle), -np.sin(angle)], axis=1)
    inverse = forward[block:].T / block
    return split(forward), split(inverse)


def params(**kw):
    return pltpu.CompilerParams(vmem_limit_bytes=60 * 1024 * 1024, **kw)


def columns(weights, rim):
    rest = jnp.zeros((128 - weights.shape[0] - rim.shape[0], weights.shape[1]), F32)
    return jnp.concatenate([weights, rim, rest], axis=0).T


def short_filter(signal, table, stream):
    signal = signal.astype(F32)
    at = lambda k: table[:, k : k + 1]
    lane = lax.broadcasted_iota(jnp.int32, signal.shape, 1)
    before2, before1 = at(16 + 2 * stream), at(17 + 2 * stream)
    lag1 = jnp.where(lane == 0, before1, pltpu.roll(signal, 1, 1))
    lag2 = jnp.where(lane == 0, before2, jnp.where(lane == 1, before1, pltpu.roll(signal, 2, 1)))
    return at(3 * stream) * signal + at(3 * stream + 1) * lag1 + at(3 * stream + 2) * lag2


def greet(count, devices):
    barrier = pltpu.get_barrier_semaphore()

    @pl.loop(1, count)
    def _(step):
        pl.semaphore_signal(barrier, inc=1, device_id=devices(step), device_id_type=MESH)

    pl.semaphore_wait(barrier, count - 1)


def settle(ref, sem):
    pltpu.make_async_copy(ref, ref, sem).wait()


def send(source, target, send_sem, recv_sem, device):
    pltpu.make_async_remote_copy(
        src_ref=source, dst_ref=target, send_sem=send_sem, recv_sem=recv_sem, device_id=device, device_id_type=MESH
    ).start()


def exchange_kernel(
    context_size, tensor_size,
    q_ref, k_ref, v_ref, own_ref, taps_ref, high_ref, low_ref,
    x_ref, spectra_ref, query_ref,
    weights_ref, edge_ref, rim_ref, products_ref, h_ref, send_sem, recv_sem,
):
    me = lax.axis_index("context")
    everyone = context_size * tensor_size
    whoami = lax.axis_index("tensor") * context_size + me
    chans = products_ref.shape[1]
    width = q_ref.shape[1]
    peer = lambda step: lax.rem(me + step, context_size)
    anyone = lambda step: lax.rem(whoami + step, everyone)
    address = lambda d: {"tensor": lax.div(d, context_size), "context": lax.rem(d, context_size)}
    greet(everyone, lambda step: address(anyone(step)))

    @pl.loop(1, context_size)
    def _(step):
        send(own_ref, weights_ref.at[me], send_sem.at[0], recv_sem.at[0], {"context": peer(step)})

    pltpu.make_async_copy(own_ref, weights_ref.at[me], recv_sem.at[0]).start()

    row = lax.broadcasted_iota(jnp.int32, (8, width), 0)
    col = lax.broadcasted_iota(jnp.int32, (8, width), 1)

    @pl.loop(0, context_size)
    def _(group):
        rows = pl.ds(pl.multiple_of(group * chans, chans), chans)
        total = jnp.zeros((8, chans), F32)
        for stream, ref in enumerate((q_ref, k_ref, v_ref)):
            pick = jnp.where(
                (row >= 2 * stream) & (row < 2 * stream + 2) & (col == width - 2 + row - 2 * stream), 1.0, 0.0
            ).astype(BF16)
            total = total + lax.dot_general(
                pick, ref[rows, :], (((1,), (1,)), ((), ())), preferred_element_type=F32
            )
        edge_ref[group] = total.astype(BF16)

    send(edge_ref, rim_ref, send_sem.at[1], recv_sem.at[1], {"context": peer(1)})

    def piece(d):
        if taps_ref.ndim == 3:
            return taps_ref.at[d]
        return taps_ref.at[:, pl.ds(pl.multiple_of(d * chans, chans), chans)]

    @pl.loop(1, everyone)
    def _(step):
        d = anyone(step)
        send(piece(d), h_ref.at[whoami], send_sem.at[2], recv_sem.at[2], address(d))

    pltpu.make_async_copy(piece(whoami), h_ref.at[whoami], recv_sem.at[2]).start()

    settle(weights_ref, recv_sem.at[0])
    settle(rim_ref, recv_sem.at[1])
    kept = jnp.where(me == 0, 0.0, 1.0).astype(F32)

    def table_of(group):
        return columns(weights_ref[group], rim_ref[group].astype(F32) * kept)

    @pl.loop(1, context_size + 1)
    def _(step):
        group = peer(step)
        rows = pl.ds(pl.multiple_of(group * chans, chans), chans)
        table = table_of(group)
        products_ref[group] = (
            short_filter(k_ref[rows, :], table, 1) * short_filter(v_ref[rows, :], table, 2)
        ).astype(BF16)

        @pl.when(step < context_size)
        def _():
            send(products_ref.at[group], x_ref.at[me], send_sem.at[3], recv_sem.at[3], {"context": group})

        @pl.when(step == context_size)
        def _():
            pltpu.make_async_copy(products_ref.at[group], x_ref.at[me], recv_sem.at[3]).start()

    @pl.loop(0, context_size)
    def _(group):
        rows = pl.ds(pl.multiple_of(group * chans, chans), chans)
        query_ref[rows, :] = short_filter(q_ref[rows, :], table_of(group), 0)

    settle(h_ref, recv_sem.at[2])
    blocks, block = spectra_ref.shape[0], spectra_ref.shape[2] // 2
    slabs = block // h_ref.shape[1]
    dims = (((0,), (0,)), ((), ()))

    @pl.loop(0, blocks)
    def _(index):
        h = jnp.concatenate([h_ref[index * slabs + part] for part in range(slabs)], axis=0)
        spectra_ref[index] = lax.dot_general(
            h, high_ref[:block], dims, preferred_element_type=F32
        ) + lax.dot_general(h, low_ref[:block], dims, preferred_element_type=F32)

    settle(weights_ref.at[pl.ds(0, context_size - 1)], send_sem.at[0])
    settle(edge_ref, send_sem.at[1])
    settle(h_ref.at[pl.ds(0, everyone - 1)], send_sem.at[2])
    settle(products_ref.at[pl.ds(0, context_size - 1)], send_sem.at[3])
    settle(x_ref, recv_sem.at[3])


def conv_kernel(
    step, x_ref, h_ref, skip_ref, high_ref, low_ref, back_high_ref, back_low_ref,
    out_ref, spec_ref, mixed_ref, sent_ref, send_sem, recv_sem,
):
    me = lax.axis_index("context")
    pieces = x_ref.shape[0]
    peer = lambda k: lax.rem(me + k, pieces)
    greet(pieces, lambda k: {"context": peer(k)})

    @pl.loop(0, x_ref.shape[1] // step)
    def _(chunk):
        rows = pl.ds(pl.multiple_of(chunk * step, step), step)
        conv_chunk(
            x_ref.at[:, rows], h_ref.at[:, rows], skip_ref.at[rows], high_ref, low_ref, back_high_ref, back_low_ref,
            sent_ref.at[:, rows], spec_ref, mixed_ref,
        )

        @pl.loop(1, pieces)
        def _(k):
            send(sent_ref.at[peer(k), rows], out_ref.at[me, rows], send_sem, recv_sem, {"context": peer(k)})

        pltpu.make_async_copy(sent_ref.at[me, rows], out_ref.at[me, rows], recv_sem).start()

    settle(sent_ref.at[pl.ds(0, pieces - 1)], send_sem)
    settle(out_ref, recv_sem)


def conv_chunk(x_ref, h_ref, skip_ref, high_ref, low_ref, back_high_ref, back_low_ref, out_ref, spec_ref, mixed_ref):
    pieces, chans, width = x_ref.shape
    blocks = pieces // 2
    half = 2 * width
    zero = jnp.zeros((chans, width), BF16)
    piece = lambda p: zero if p < 0 else x_ref[p]
    parts = [jnp.concatenate([piece(2 * j - 2 + lag) for j in range(blocks)], axis=0) for lag in range(4)]
    stacked = jnp.concatenate(parts, axis=1)
    spec_ref[...] = jnp.dot(stacked, high_ref[...], preferred_element_type=F32) + jnp.dot(
        stacked, low_ref[...], preferred_element_type=F32
    )

    @pl.loop(0, chans // 8)
    def _(group):
        base = pl.multiple_of(group * 8, 8)
        for lanes in range(half // 128):
            real, imag = pl.ds(lanes * 128, 128), pl.ds(half + lanes * 128, 128)
            rows = [pl.ds(pl.multiple_of(j * chans + base, 8), 8) for j in range(blocks)]
            xr = [spec_ref[r, real] for r in rows]
            xi = [spec_ref[r, imag] for r in rows]
            hr = [h_ref[j, pl.ds(base, 8), real] for j in range(blocks)]
            hi = [h_ref[j, pl.ds(base, 8), imag] for j in range(blocks)]
            for i in range(blocks):
                yr = xr[i] * hr[0] - xi[i] * hi[0]
                yi = xr[i] * hi[0] + xi[i] * hr[0]
                for j in range(i):
                    d = i - j
                    yr = yr + xr[j] * hr[d] - xi[j] * hi[d]
                    yi = yi + xr[j] * hi[d] + xi[j] * hr[d]
                mixed_ref[rows[i], real] = yr
                mixed_ref[rows[i], imag] = yi

    spectrum = mixed_ref[...]
    top = spectrum.astype(BF16)
    rest = (spectrum - top.astype(F32)).astype(BF16)
    conv = (
        jnp.dot(top, back_high_ref[...], preferred_element_type=F32)
        + jnp.dot(rest, back_high_ref[...], preferred_element_type=F32)
        + jnp.dot(top, back_low_ref[...], preferred_element_type=F32)
    )
    skip = skip_ref[...]
    for j in range(blocks):
        for side in range(2):
            part = conv[j * chans : (j + 1) * chans, side * width : (side + 1) * width]
            out_ref[2 * j + side] = (part + skip * x_ref[2 * j + side].astype(F32)).astype(BF16)


def local(query_stream, key_stream, value_stream, filter_taps, short_filters, skip_gain):
    group_width, block_rows = query_stream.shape
    context_size = lax.axis_size("context")
    tensor_size = lax.axis_size("tensor")
    everyone = tensor_size * context_size
    chans = group_width // context_size
    offset_rows = filter_taps.shape[0]
    block = 2 * block_rows
    blocks = context_size // 2
    (high, low), (back_high, back_low) = tables(block)

    vmem = pl.BlockSpec(memory_space=pltpu.VMEM)
    weights = jnp.pad(short_filters.reshape(9, chans), ((0, 7), (0, 0)))
    taps = filter_taps
    if chans % 128:
        taps = taps.reshape(offset_rows, everyone, chans).transpose(1, 0, 2)
    pieces = (context_size, chans, block_rows)
    dma = pltpu.SemaphoreType.DMA
    arrived, spectra, query_short = pl.pallas_call(
        functools.partial(exchange_kernel, context_size, tensor_size),
        in_specs=[vmem] * 4 + [pl.BlockSpec(memory_space=pl.ANY)] + [vmem] * 2,
        out_specs=[vmem] * 3,
        out_shape=[
            jax.ShapeDtypeStruct(pieces, BF16),
            jax.ShapeDtypeStruct((blocks, chans, 2 * block), F32),
            jax.ShapeDtypeStruct((group_width, block_rows), F32),
        ],
        scratch_shapes=[
            pltpu.VMEM((context_size, 16, chans), F32),
            pltpu.VMEM((context_size, 8, chans), BF16),
            pltpu.VMEM((context_size, 8, chans), BF16),
            pltpu.VMEM(pieces, BF16),
            pltpu.VMEM((everyone, offset_rows, chans), BF16),
            dma((4,)),
            dma((4,)),
        ],
        compiler_params=params(collective_id=0, has_side_effects=True),
    )(query_stream, key_stream, value_stream, weights, taps, high, low)

    step = min(chans, 64)
    returned = pl.pallas_call(
        functools.partial(conv_kernel, step),
        in_specs=[vmem] * 7,
        out_specs=vmem,
        out_shape=jax.ShapeDtypeStruct(pieces, BF16),
        scratch_shapes=[pltpu.VMEM((blocks * step, 2 * block), F32)] * 2
        + [pltpu.VMEM(pieces, BF16), dma, dma],
        compiler_params=params(collective_id=1, has_side_effects=True),
    )(arrived, spectra, skip_gain[:, None], high, low, back_high, back_low)
    return (query_short * returned.reshape(group_width, block_rows).astype(F32)).astype(BF16)


def solution(mesh):
    placed = (
        P("tensor", "context"),
        P("tensor", "context"),
        P("tensor", "context"),
        P(("tensor", "context"), None),
        P(None, None, ("tensor", "context")),
        P(("tensor", "context")),
    )
    return jax.shard_map(
        local, mesh=mesh, in_specs=placed, out_specs=P("tensor", "context"), check_vma=False
    )
```

```python
import functools

import jax
import jax.numpy as jnp
import ml_dtypes
import numpy as np
from jax import lax
from jax.experimental import pallas as pl
from jax.experimental.pallas import tpu as pltpu
from jax.sharding import PartitionSpec as P

F32, BF16 = jnp.float32, jnp.bfloat16
MESH = pl.DeviceIdType.MESH


def split(table):
    high = table.astype(ml_dtypes.bfloat16)
    low = (table - high.astype(np.float64)).astype(ml_dtypes.bfloat16)
    return jnp.asarray(high), jnp.asarray(low)


def tables(block):
    n = np.arange(2 * block)
    f = np.arange(block)
    phase = (n[:, None] * (2 * f[None, :] + 1)) % (4 * block)
    angle = phase * (2.0 * np.pi / (4 * block))
    forward = np.concatenate([np.cos(angle), -np.sin(angle)], axis=1)
    inverse = forward[block:].T / block
    return split(forward), split(inverse)


def params(**kw):
    return pltpu.CompilerParams(vmem_limit_bytes=60 * 1024 * 1024, **kw)


def columns(weights, rim):
    rest = jnp.zeros((128 - weights.shape[0] - rim.shape[0], weights.shape[1]), F32)
    return jnp.concatenate([weights, rim, rest], axis=0).T


def short_filter(signal, table, stream):
    signal = signal.astype(F32)
    at = lambda k: table[:, k : k + 1]
    lane = lax.broadcasted_iota(jnp.int32, signal.shape, 1)
    before2, before1 = at(16 + 2 * stream), at(17 + 2 * stream)
    lag1 = jnp.where(lane == 0, before1, pltpu.roll(signal, 1, 1))
    lag2 = jnp.where(lane == 0, before2, jnp.where(lane == 1, before1, pltpu.roll(signal, 2, 1)))
    return at(3 * stream) * signal + at(3 * stream + 1) * lag1 + at(3 * stream + 2) * lag2


def greet(count, devices):
    barrier = pltpu.get_barrier_semaphore()

    @pl.loop(1, count)
    def _(step):
        pl.semaphore_signal(barrier, inc=1, device_id=devices(step), device_id_type=MESH)

    pl.semaphore_wait(barrier, count - 1)


def settle(ref, sem):
    pltpu.make_async_copy(ref, ref, sem).wait()


def send(source, target, send_sem, recv_sem, device):
    pltpu.make_async_remote_copy(
        src_ref=source, dst_ref=target, send_sem=send_sem, recv_sem=recv_sem, device_id=device, device_id_type=MESH
    ).start()


def operator_kernel(
    context_size, tensor_size, depth,
    q_ref, k_ref, v_ref, short_ref, skip_ref, taps_ref, high_ref, low_ref, back_high_ref, back_low_ref,
    out_ref,
    own_ref, weights_ref, edge_ref, rim_ref, products_ref, h_ref, x_ref, spectra_ref, query_ref, gain_ref,
    spec_ref, mixed_ref, sent_ref, back_ref, send_sem, recv_sem, chunk_sem, back_sem,
):
    me = lax.axis_index("context")
    everyone = context_size * tensor_size
    whoami = lax.axis_index("tensor") * context_size + me
    chans = products_ref.shape[1]
    width = q_ref.shape[1]
    peer = lambda step: lax.rem(me + step, context_size)
    anyone = lambda step: lax.rem(whoami + step, everyone)
    address = lambda d: {"tensor": lax.div(d, context_size), "context": lax.rem(d, context_size)}
    greet(everyone, lambda step: address(anyone(step)))

    own_ref[...] = jnp.zeros_like(own_ref)
    for stream in range(3):
        for lag in range(3):
            own_ref[3 * stream + lag] = short_ref[stream, lag]

    @pl.loop(1, context_size)
    def _(step):
        send(own_ref, weights_ref.at[me], send_sem.at[0], recv_sem.at[0], {"context": peer(step)})

    pltpu.make_async_copy(own_ref, weights_ref.at[me], recv_sem.at[0]).start()

    row = lax.broadcasted_iota(jnp.int32, (8, width), 0)
    col = lax.broadcasted_iota(jnp.int32, (8, width), 1)

    @pl.loop(0, context_size)
    def _(group):
        rows = pl.ds(pl.multiple_of(group * chans, chans), chans)
        total = jnp.zeros((8, chans), F32)
        for stream, ref in enumerate((q_ref, k_ref, v_ref)):
            pick = jnp.where(
                (row >= 2 * stream) & (row < 2 * stream + 2) & (col == width - 2 + row - 2 * stream), 1.0, 0.0
            ).astype(BF16)
            total = total + lax.dot_general(
                pick, ref[rows, :], (((1,), (1,)), ((), ())), preferred_element_type=F32
            )
        edge_ref[group] = total.astype(BF16)

    send(edge_ref, rim_ref, send_sem.at[1], recv_sem.at[1], {"context": peer(1)})

    def piece(d):
        if taps_ref.ndim == 3:
            return taps_ref.at[d]
        return taps_ref.at[:, pl.ds(pl.multiple_of(d * chans, chans), chans)]

    @pl.loop(1, everyone)
    def _(step):
        d = anyone(step)
        send(piece(d), h_ref.at[whoami], send_sem.at[2], recv_sem.at[2], address(d))

    pltpu.make_async_copy(piece(whoami), h_ref.at[whoami], recv_sem.at[2]).start()

    settle(weights_ref, recv_sem.at[0])
    settle(rim_ref, recv_sem.at[1])
    kept = jnp.where(me == 0, 0.0, 1.0).astype(F32)

    def table_of(group):
        return columns(weights_ref[group], rim_ref[group].astype(F32) * kept)

    @pl.loop(1, context_size + 1)
    def _(step):
        group = peer(step)
        rows = pl.ds(pl.multiple_of(group * chans, chans), chans)
        table = table_of(group)
        products_ref[group] = (
            short_filter(k_ref[rows, :], table, 1) * short_filter(v_ref[rows, :], table, 2)
        ).astype(BF16)

    chunks = chans // depth
    chunk_rows = lambda chunk: pl.ds(pl.multiple_of(chunk * depth, depth), depth)

    @pl.loop(0, chunks)
    def _(chunk):
        rows = chunk_rows(chunk)

        @pl.loop(1, context_size)
        def _(step):
            group = peer(step)
            send(
                products_ref.at[group, rows], x_ref.at[me, rows], send_sem.at[3], chunk_sem.at[chunk], {"context": group}
            )

        pltpu.make_async_copy(products_ref.at[me, rows], x_ref.at[me, rows], chunk_sem.at[chunk]).start()

    gain = jnp.concatenate([skip_ref[...], jnp.zeros((127, chans), F32)], axis=0)
    gain_ref[...] = gain.T

    @pl.loop(0, context_size)
    def _(group):
        rows = pl.ds(pl.multiple_of(group * chans, chans), chans)
        query_ref[rows, :] = short_filter(q_ref[rows, :], table_of(group), 0)

    settle(h_ref, recv_sem.at[2])
    blocks, block = spectra_ref.shape[0], spectra_ref.shape[2] // 2
    slabs = block // h_ref.shape[1]
    dims = (((0,), (0,)), ((), ()))

    @pl.loop(0, blocks)
    def _(index):
        h = jnp.concatenate([h_ref[index * slabs + part] for part in range(slabs)], axis=0)
        spectra_ref[index] = lax.dot_general(
            h, high_ref[:block], dims, preferred_element_type=F32
        ) + lax.dot_general(h, low_ref[:block], dims, preferred_element_type=F32)

    @pl.loop(0, chunks)
    def _(chunk):
        rows = chunk_rows(chunk)
        settle(x_ref.at[:, rows], chunk_sem.at[chunk])
        conv_chunk(
            x_ref.at[:, rows], spectra_ref.at[:, rows], gain_ref.at[rows], high_ref, low_ref, back_high_ref,
            back_low_ref, sent_ref.at[:, rows], spec_ref, mixed_ref,
        )

        @pl.loop(1, context_size)
        def _(step):
            group = peer(step)
            send(sent_ref.at[group, rows], back_ref.at[me, rows], send_sem.at[4], back_sem.at[chunk], {"context": group})

        pltpu.make_async_copy(sent_ref.at[me, rows], back_ref.at[me, rows], back_sem.at[chunk]).start()

    @pl.loop(0, chunks)
    def _(chunk):
        rows = chunk_rows(chunk)
        settle(back_ref.at[:, rows], back_sem.at[chunk])

        @pl.loop(0, context_size)
        def _(group):
            flat = pl.ds(pl.multiple_of(group * chans + chunk * depth, depth), depth)
            out_ref[flat, :] = (query_ref[flat, :] * back_ref[group, rows].astype(F32)).astype(BF16)

    settle(weights_ref.at[pl.ds(0, context_size - 1)], send_sem.at[0])
    settle(edge_ref, send_sem.at[1])
    settle(h_ref.at[pl.ds(0, everyone - 1)], send_sem.at[2])
    settle(products_ref.at[pl.ds(0, context_size - 1)], send_sem.at[3])
    settle(sent_ref.at[pl.ds(0, context_size - 1)], send_sem.at[4])


def conv_chunk(x_ref, h_ref, skip_ref, high_ref, low_ref, back_high_ref, back_low_ref, out_ref, spec_ref, mixed_ref):
    pieces, chans, width = x_ref.shape
    blocks = pieces // 2
    half = 2 * width
    zero = jnp.zeros((chans, width), BF16)
    piece = lambda p: zero if p < 0 else x_ref[p]
    parts = [jnp.concatenate([piece(2 * j - 2 + lag) for j in range(blocks)], axis=0) for lag in range(4)]
    stacked = jnp.concatenate(parts, axis=1)
    spec_ref[...] = jnp.dot(stacked, high_ref[...], preferred_element_type=F32) + jnp.dot(
        stacked, low_ref[...], preferred_element_type=F32
    )

    @pl.loop(0, chans // 8)
    def _(group):
        base = pl.multiple_of(group * 8, 8)
        for lanes in range(half // 128):
            real, imag = pl.ds(lanes * 128, 128), pl.ds(half + lanes * 128, 128)
            rows = [pl.ds(pl.multiple_of(j * chans + base, 8), 8) for j in range(blocks)]
            xr = [spec_ref[r, real] for r in rows]
            xi = [spec_ref[r, imag] for r in rows]
            hr = [h_ref[j, pl.ds(base, 8), real] for j in range(blocks)]
            hi = [h_ref[j, pl.ds(base, 8), imag] for j in range(blocks)]
            for i in range(blocks):
                yr = xr[i] * hr[0] - xi[i] * hi[0]
                yi = xr[i] * hi[0] + xi[i] * hr[0]
                for j in range(i):
                    d = i - j
                    yr = yr + xr[j] * hr[d] - xi[j] * hi[d]
                    yi = yi + xr[j] * hi[d] + xi[j] * hr[d]
                mixed_ref[rows[i], real] = yr
                mixed_ref[rows[i], imag] = yi

    spectrum = mixed_ref[...]
    top = spectrum.astype(BF16)
    rest = (spectrum - top.astype(F32)).astype(BF16)
    conv = (
        jnp.dot(top, back_high_ref[...], preferred_element_type=F32)
        + jnp.dot(rest, back_high_ref[...], preferred_element_type=F32)
        + jnp.dot(top, back_low_ref[...], preferred_element_type=F32)
    )
    skip = skip_ref[:, :1]
    for j in range(blocks):
        for side in range(2):
            part = conv[j * chans : (j + 1) * chans, side * width : (side + 1) * width]
            out_ref[2 * j + side] = (part + skip * x_ref[2 * j + side].astype(F32)).astype(BF16)


def local(query_stream, key_stream, value_stream, filter_taps, short_filters, skip_gain):
    group_width, block_rows = query_stream.shape
    context_size = lax.axis_size("context")
    tensor_size = lax.axis_size("tensor")
    everyone = tensor_size * context_size
    chans = group_width // context_size
    offset_rows = filter_taps.shape[0]
    block = 2 * block_rows
    blocks = context_size // 2
    (high, low), (back_high, back_low) = tables(block)

    vmem = pl.BlockSpec(memory_space=pltpu.VMEM)
    taps = filter_taps
    if chans % 128:
        taps = taps.reshape(offset_rows, everyone, chans).transpose(1, 0, 2)
    depth = min(chans, 64)
    chunks = chans // depth
    pieces = pltpu.VMEM((context_size, chans, block_rows), BF16)
    dma = pltpu.SemaphoreType.DMA
    return pl.pallas_call(
        functools.partial(operator_kernel, context_size, tensor_size, depth),
        in_specs=[vmem] * 5 + [pl.BlockSpec(memory_space=pl.ANY)] + [vmem] * 4,
        out_specs=vmem,
        out_shape=jax.ShapeDtypeStruct((group_width, block_rows), BF16),
        scratch_shapes=[
            pltpu.VMEM((16, chans), F32),
            pltpu.VMEM((context_size, 16, chans), F32),
            pltpu.VMEM((context_size, 8, chans), BF16),
            pltpu.VMEM((context_size, 8, chans), BF16),
            pieces,
            pltpu.VMEM((everyone, offset_rows, chans), BF16),
            pieces,
            pltpu.VMEM((blocks, chans, 2 * block), F32),
            pltpu.VMEM((group_width, block_rows), F32),
            pltpu.VMEM((chans, 128), F32),
            pltpu.VMEM((blocks * depth, 2 * block), F32),
            pltpu.VMEM((blocks * depth, 2 * block), F32),
            pieces,
            pieces,
            dma((5,)),
            dma((3,)),
            dma((chunks,)),
            dma((chunks,)),
        ],
        compiler_params=params(collective_id=0, has_side_effects=True),
    )(
        query_stream, key_stream, value_stream, short_filters, skip_gain[None, :], taps,
        high, low, back_high, back_low,
    )


def solution(mesh):
    placed = (
        P("tensor", "context"),
        P("tensor", "context"),
        P("tensor", "context"),
        P(("tensor", "context"), None),
        P(None, None, ("tensor", "context")),
        P(("tensor", "context")),
    )
    return jax.shard_map(
        local, mesh=mesh, in_specs=placed, out_specs=P("tensor", "context"), check_vma=False
    )
```

```python
import functools

import jax
import jax.numpy as jnp
import ml_dtypes
import numpy as np
from jax import lax
from jax.experimental import pallas as pl
from jax.experimental.pallas import tpu as pltpu
from jax.sharding import PartitionSpec as P

F32, BF16 = jnp.float32, jnp.bfloat16
MESH = pl.DeviceIdType.MESH


def split(table):
    high = table.astype(ml_dtypes.bfloat16)
    low = (table - high.astype(np.float64)).astype(ml_dtypes.bfloat16)
    return jnp.asarray(high), jnp.asarray(low)


def tables(block):
    n = np.arange(2 * block)
    f = np.arange(block)
    phase = (n[:, None] * (2 * f[None, :] + 1)) % (4 * block)
    angle = phase * (2.0 * np.pi / (4 * block))
    forward = np.concatenate([np.cos(angle), -np.sin(angle)], axis=1)
    inverse = forward[block:].T / block
    return split(forward), split(inverse)


def params(**kw):
    return pltpu.CompilerParams(vmem_limit_bytes=60 * 1024 * 1024, **kw)


def columns(weights, rim):
    rest = jnp.zeros((128 - weights.shape[0] - rim.shape[0], weights.shape[1]), F32)
    return jnp.concatenate([weights, rim, rest], axis=0).T


def short_filter(signal, table, stream):
    signal = signal.astype(F32)
    at = lambda k: table[:, k : k + 1]
    lane = lax.broadcasted_iota(jnp.int32, signal.shape, 1)
    before2, before1 = at(16 + 2 * stream), at(17 + 2 * stream)
    lag1 = jnp.where(lane == 0, before1, pltpu.roll(signal, 1, 1))
    lag2 = jnp.where(lane == 0, before2, jnp.where(lane == 1, before1, pltpu.roll(signal, 2, 1)))
    return at(3 * stream) * signal + at(3 * stream + 1) * lag1 + at(3 * stream + 2) * lag2


def greet(count, devices):
    barrier = pltpu.get_barrier_semaphore()

    @pl.loop(1, count)
    def _(step):
        pl.semaphore_signal(barrier, inc=1, device_id=devices(step), device_id_type=MESH)

    pl.semaphore_wait(barrier, count - 1)


def settle(ref, sem):
    pltpu.make_async_copy(ref, ref, sem).wait()


def send(source, target, send_sem, recv_sem, device):
    pltpu.make_async_remote_copy(
        src_ref=source, dst_ref=target, send_sem=send_sem, recv_sem=recv_sem, device_id=device, device_id_type=MESH
    ).start()


def operator_kernel(
    context_size, tensor_size, depth,
    q_ref, k_ref, v_ref, short_ref, skip_ref, taps_ref, high_ref, low_ref, back_high_ref, back_low_ref,
    out_ref,
    own_ref, weights_ref, edge_ref, rim_ref, products_ref, h_ref, x_ref, spectra_ref, query_ref, gain_ref,
    spec_ref, mixed_ref, sent_ref, back_ref, send_sem, recv_sem, chunk_sem, back_sem,
):
    me = lax.axis_index("context")
    everyone = context_size * tensor_size
    whoami = lax.axis_index("tensor") * context_size + me
    chans = products_ref.shape[1]
    width = q_ref.shape[1]
    peer = lambda step: lax.rem(me + step, context_size)
    anyone = lambda step: lax.rem(whoami + step, everyone)
    address = lambda d: {"tensor": lax.div(d, context_size), "context": lax.rem(d, context_size)}
    greet(everyone, lambda step: address(anyone(step)))

    own_ref[...] = jnp.zeros_like(own_ref)
    for stream in range(3):
        for lag in range(3):
            own_ref[3 * stream + lag] = short_ref[stream, lag]

    @pl.loop(1, context_size)
    def _(step):
        send(own_ref, weights_ref.at[me], send_sem.at[0], recv_sem.at[0], {"context": peer(step)})

    pltpu.make_async_copy(own_ref, weights_ref.at[me], recv_sem.at[0]).start()

    row = lax.broadcasted_iota(jnp.int32, (8, width), 0)
    col = lax.broadcasted_iota(jnp.int32, (8, width), 1)

    @pl.loop(0, context_size)
    def _(group):
        rows = pl.ds(pl.multiple_of(group * chans, chans), chans)
        total = jnp.zeros((8, chans), F32)
        for stream, ref in enumerate((q_ref, k_ref, v_ref)):
            pick = jnp.where(
                (row >= 2 * stream) & (row < 2 * stream + 2) & (col == width - 2 + row - 2 * stream), 1.0, 0.0
            ).astype(BF16)
            total = total + lax.dot_general(
                pick, ref[rows, :], (((1,), (1,)), ((), ())), preferred_element_type=F32
            )
        edge_ref[group] = total.astype(BF16)

    send(edge_ref, rim_ref, send_sem.at[1], recv_sem.at[1], {"context": peer(1)})

    def piece(d):
        if taps_ref.ndim == 3:
            return taps_ref.at[d]
        return taps_ref.at[:, pl.ds(pl.multiple_of(d * chans, chans), chans)]

    @pl.loop(1, everyone)
    def _(step):
        d = anyone(step)
        send(piece(d), h_ref.at[whoami], send_sem.at[2], recv_sem.at[2], address(d))

    pltpu.make_async_copy(piece(whoami), h_ref.at[whoami], recv_sem.at[2]).start()

    settle(weights_ref, recv_sem.at[0])
    settle(rim_ref, recv_sem.at[1])
    kept = jnp.where(me == 0, 0.0, 1.0).astype(F32)

    def table_of(group):
        return columns(weights_ref[group], rim_ref[group].astype(F32) * kept)

    @pl.loop(1, context_size + 1)
    def _(step):
        group = peer(step)
        rows = pl.ds(pl.multiple_of(group * chans, chans), chans)
        table = table_of(group)
        products_ref[group] = (
            short_filter(k_ref[rows, :], table, 1) * short_filter(v_ref[rows, :], table, 2)
        ).astype(BF16)

    chunks = chans // depth
    chunk_rows = lambda chunk: pl.ds(pl.multiple_of(chunk * depth, depth), depth)

    @pl.loop(0, chunks)
    def _(chunk):
        rows = chunk_rows(chunk)

        @pl.loop(1, context_size)
        def _(step):
            group = peer(step)
            send(
                products_ref.at[group, rows], x_ref.at[me, rows], send_sem.at[3], chunk_sem.at[chunk], {"context": group}
            )

        pltpu.make_async_copy(products_ref.at[me, rows], x_ref.at[me, rows], chunk_sem.at[chunk]).start()

    gain = jnp.concatenate([skip_ref[...], jnp.zeros((127, chans), F32)], axis=0)
    gain_ref[...] = gain.T

    @pl.loop(0, context_size)
    def _(group):
        rows = pl.ds(pl.multiple_of(group * chans, chans), chans)
        query_ref[rows, :] = short_filter(q_ref[rows, :], table_of(group), 0)

    settle(h_ref, recv_sem.at[2])
    blocks, block = spectra_ref.shape[0], spectra_ref.shape[2] // 2
    slabs = block // h_ref.shape[1]
    dims = (((0,), (0,)), ((), ()))

    @pl.loop(0, blocks)
    def _(index):
        h = jnp.concatenate([h_ref[index * slabs + part] for part in range(slabs)], axis=0)
        spectra_ref[index] = lax.dot_general(
            h, high_ref[:block], dims, preferred_element_type=F32
        ) + lax.dot_general(h, low_ref[:block], dims, preferred_element_type=F32)

    @pl.loop(0, chunks)
    def _(chunk):
        rows = chunk_rows(chunk)
        settle(x_ref.at[:, rows], chunk_sem.at[chunk])
        conv_chunk(
            x_ref.at[:, rows], spectra_ref.at[:, rows], gain_ref.at[rows], high_ref, low_ref, back_high_ref,
            back_low_ref, sent_ref.at[:, rows], spec_ref, mixed_ref,
        )

        @pl.loop(1, context_size)
        def _(step):
            group = peer(step)
            send(sent_ref.at[group, rows], back_ref.at[me, rows], send_sem.at[4], back_sem.at[chunk], {"context": group})

        pltpu.make_async_copy(sent_ref.at[me, rows], back_ref.at[me, rows], back_sem.at[chunk]).start()

    @pl.loop(0, chunks)
    def _(chunk):
        rows = chunk_rows(chunk)
        settle(back_ref.at[:, rows], back_sem.at[chunk])

        @pl.loop(0, context_size)
        def _(group):
            flat = pl.ds(pl.multiple_of(group * chans + chunk * depth, depth), depth)
            out_ref[flat, :] = (query_ref[flat, :] * back_ref[group, rows].astype(F32)).astype(BF16)

    settle(weights_ref.at[pl.ds(0, context_size - 1)], send_sem.at[0])
    settle(edge_ref, send_sem.at[1])
    settle(h_ref.at[pl.ds(0, everyone - 1)], send_sem.at[2])
    settle(products_ref.at[pl.ds(0, context_size - 1)], send_sem.at[3])
    settle(sent_ref.at[pl.ds(0, context_size - 1)], send_sem.at[4])


def conv_chunk(x_ref, h_ref, skip_ref, high_ref, low_ref, back_high_ref, back_low_ref, out_ref, spec_ref, mixed_ref):
    pieces, chans, width = x_ref.shape
    blocks = pieces // 2
    half = 2 * width
    zero = jnp.zeros((chans, width), BF16)
    piece = lambda p: zero if p < 0 else x_ref[p]
    parts = [jnp.concatenate([piece(2 * j - 2 + lag) for j in range(blocks)], axis=0) for lag in range(4)]
    stacked = jnp.concatenate(parts, axis=1)
    spec_ref[...] = jnp.dot(stacked, high_ref[...], preferred_element_type=F32)

    @pl.loop(0, chans // 8)
    def _(group):
        base = pl.multiple_of(group * 8, 8)
        for lanes in range(half // 128):
            real, imag = pl.ds(lanes * 128, 128), pl.ds(half + lanes * 128, 128)
            rows = [pl.ds(pl.multiple_of(j * chans + base, 8), 8) for j in range(blocks)]
            xr = [spec_ref[r, real] for r in rows]
            xi = [spec_ref[r, imag] for r in rows]
            hr = [h_ref[j, pl.ds(base, 8), real] for j in range(blocks)]
            hi = [h_ref[j, pl.ds(base, 8), imag] for j in range(blocks)]
            for i in range(blocks):
                yr = xr[i] * hr[0] - xi[i] * hi[0]
                yi = xr[i] * hi[0] + xi[i] * hr[0]
                for j in range(i):
                    d = i - j
                    yr = yr + xr[j] * hr[d] - xi[j] * hi[d]
                    yi = yi + xr[j] * hi[d] + xi[j] * hr[d]
                mixed_ref[rows[i], real] = yr
                mixed_ref[rows[i], imag] = yi

    spectrum = mixed_ref[...]
    top = spectrum.astype(BF16)
    rest = (spectrum - top.astype(F32)).astype(BF16)
    conv = (
        jnp.dot(top, back_high_ref[...], preferred_element_type=F32)
        + jnp.dot(rest, back_high_ref[...], preferred_element_type=F32)
        + jnp.dot(top, back_low_ref[...], preferred_element_type=F32)
    )
    skip = skip_ref[:, :1]
    for j in range(blocks):
        for side in range(2):
            part = conv[j * chans : (j + 1) * chans, side * width : (side + 1) * width]
            out_ref[2 * j + side] = (part + skip * x_ref[2 * j + side].astype(F32)).astype(BF16)


def local(query_stream, key_stream, value_stream, filter_taps, short_filters, skip_gain):
    group_width, block_rows = query_stream.shape
    context_size = lax.axis_size("context")
    tensor_size = lax.axis_size("tensor")
    everyone = tensor_size * context_size
    chans = group_width // context_size
    offset_rows = filter_taps.shape[0]
    block = 2 * block_rows
    blocks = context_size // 2
    (high, low), (back_high, back_low) = tables(block)

    vmem = pl.BlockSpec(memory_space=pltpu.VMEM)
    taps = filter_taps
    if chans % 128:
        taps = taps.reshape(offset_rows, everyone, chans).transpose(1, 0, 2)
    depth = min(chans, 64)
    chunks = chans // depth
    pieces = pltpu.VMEM((context_size, chans, block_rows), BF16)
    dma = pltpu.SemaphoreType.DMA
    return pl.pallas_call(
        functools.partial(operator_kernel, context_size, tensor_size, depth),
        in_specs=[vmem] * 5 + [pl.BlockSpec(memory_space=pl.ANY)] + [vmem] * 4,
        out_specs=vmem,
        out_shape=jax.ShapeDtypeStruct((group_width, block_rows), BF16),
        scratch_shapes=[
            pltpu.VMEM((16, chans), F32),
            pltpu.VMEM((context_size, 16, chans), F32),
            pltpu.VMEM((context_size, 8, chans), BF16),
            pltpu.VMEM((context_size, 8, chans), BF16),
            pieces,
            pltpu.VMEM((everyone, offset_rows, chans), BF16),
            pieces,
            pltpu.VMEM((blocks, chans, 2 * block), F32),
            pltpu.VMEM((group_width, block_rows), F32),
            pltpu.VMEM((chans, 128), F32),
            pltpu.VMEM((blocks * depth, 2 * block), F32),
            pltpu.VMEM((blocks * depth, 2 * block), F32),
            pieces,
            pieces,
            dma((5,)),
            dma((3,)),
            dma((chunks,)),
            dma((chunks,)),
        ],
        compiler_params=params(collective_id=0, has_side_effects=True),
    )(
        query_stream, key_stream, value_stream, short_filters, skip_gain[None, :], taps,
        high, low, back_high, back_low,
    )


def solution(mesh):
    placed = (
        P("tensor", "context"),
        P("tensor", "context"),
        P("tensor", "context"),
        P(("tensor", "context"), None),
        P(None, None, ("tensor", "context")),
        P(("tensor", "context")),
    )
    return jax.shard_map(
        local, mesh=mesh, in_specs=placed, out_specs=P("tensor", "context"), check_vma=False
    )
```
